32 devices in a mesh: slab: 2 (over x), gal: 4 (over y, core), qb: 4 (over z).
Axes of the slice: x: 2, y: 2, z: 4, core: 2. Of those that a mesh axis runs over, the one named last changes fastest.
Arguments:
- gallery: bfloat16 [16384, 768], P(('slab', 'gal')), parts along dimension 0, may hold values from -512 to 512
- querybank: bfloat16 [8, 2048, 768], P(('slab', 'qb'), 'gal'), parts along dimension 0, may hold values from -512 to 512
- test_queries: bfloat16 [8, 512, 768], P(('slab', 'qb'), 'gal'), parts along dimension 0, may hold values from -512 to 512
Outputs:
- logprob: float32 [4096, 8192], P(('slab', 'qb'), 'gal'), parts along dimension 0
- normalizer: float32 [16384], P(('slab', 'gal')), parts along dimension 0
The draws below stay inside these ranges and needn't reach their ends.
There are 2 independent parts, one for each index of `slab`. The reference program is written for one: setup_inputs(seed, part) draws one part's arguments, and reference() takes and returns one part's arrays. A program takes and returns all parts, laid end to end along the dimension named above; each array names one. Nothing has to cross between parts.
All inputs are finite; a program needn't handle non-finite values.
Results may differ from the reference program's by a relative error of at most 0.00049.
Values may be sent and summed in bfloat16 or wider, within the bound.
No kernel may reach another device: no remote copies, remote signals or barrier semaphores. Data moves between devices by JAX's collectives and lax.ppermute only.
A program may use at most 64 MiB of HBM per device.

```python
import math
import jax
import jax.numpy as jnp
from jax import lax

D = 768
QB_DEV = 2048
GAL_DEV = 2048
TEST_DEV = 512
CLUSTERS = 256
QB_GROUPS = 4
QBANK = 8192
GALLERY = 8192
TEST = 2048


def shared_parts(key):
    base = jax.random.fold_in(key, 11)
    centers = jnp.clip(jax.random.normal(jax.random.fold_in(base, 1), (CLUSTERS, D), jnp.float32), -4.0, 4.0)
    feature = jnp.exp(jax.random.uniform(jax.random.fold_in(base, 2), (D,), jnp.float32, 0.0, math.log(10.0)))
    return (centers, feature)


def embed_rows(key, rows, salt):
    centers, feature = shared_parts(key)
    own = jax.random.fold_in(key, salt)
    cluster = jax.random.randint(jax.random.fold_in(own, 1), (rows,), 0, CLUSTERS)
    noise = jnp.clip(jax.random.normal(jax.random.fold_in(own, 2), (rows, D), jnp.float32), -4.0, 4.0)
    center_weight, noise_weight = (0.74, 0.67)
    mixed = center_weight * centers[cluster] + noise_weight * noise
    scale = jnp.exp(jax.random.uniform(jax.random.fold_in(own, 3), (rows, 1), jnp.float32, 0.0, math.log(10.0)))
    return jnp.clip(scale * feature[None, :] * mixed, -512.0, 512.0)


def draw_gallery(key, part):
    return embed_rows(key, GALLERY, 21).astype(jnp.bfloat16)


def draw_querybank(key, part):
    return embed_rows(key, QB_GROUPS * QB_DEV, 22).reshape(QB_GROUPS, QB_DEV, D).astype(jnp.bfloat16)


def draw_test_queries(key, part):
    return embed_rows(key, QB_GROUPS * TEST_DEV, 23).reshape(QB_GROUPS, TEST_DEV, D).astype(jnp.bfloat16)


def setup_inputs(seed: int = 0, part: int = 0) -> dict:
    key_of = jax.random.split(jax.random.key(seed), 4)
    part_splits = jax.random.split(jax.random.fold_in(key_of[3], part), 4)
    return {
        "gallery": draw_gallery(jax.random.fold_in(jax.random.fold_in(key_of[3], part), 71), part),
        "querybank": draw_querybank(jax.random.fold_in(jax.random.fold_in(key_of[3], part), 71), part),
        "test_queries": draw_test_queries(jax.random.fold_in(jax.random.fold_in(key_of[3], part), 71), part),
    }


sharpness = 20.0

def unit_rows(values):
    wide = values.astype(jnp.float32)
    scaled = wide * lax.rsqrt(lax.optimization_barrier(jnp.sum(wide * wide, axis=-1, keepdims=True)) + 1e-06)
    return scaled.astype(jnp.bfloat16)

def reference(gallery, querybank, test_queries):
    gallery_unit = unit_rows(gallery)
    bank_unit = unit_rows(querybank.reshape(QBANK, D))
    test_unit = unit_rows(test_queries.reshape(TEST, D))
    blocks = gallery_unit.reshape(GALLERY // GAL_DEV, GAL_DEV, D)

    def column_block(block):
        scores = jnp.dot(bank_unit, block.T, preferred_element_type=jnp.float32)
        return lax.optimization_barrier(jnp.sum(jnp.exp(sharpness * (scores - 1.0)), axis=0))
    column_total = lax.map(column_block, blocks).reshape(GALLERY)
    normalizer = sharpness + jnp.log(column_total)
    offset = 2.0 * sharpness - math.log(QBANK)
    scores = jnp.dot(test_unit, gallery_unit.T, preferred_element_type=jnp.float32)
    logits = sharpness * scores - normalizer[None, :] - offset
    row_total = lax.optimization_barrier(jnp.sum(jnp.exp(logits), axis=1, keepdims=True))
    logprob = logits - jnp.log(row_total)
    return (logprob, normalizer)
```

```python
import functools
import math

import jax
import jax.numpy as jnp
from jax import lax
from jax.experimental import pallas as pl
from jax.experimental.pallas import tpu as pltpu
from jax.sharding import PartitionSpec as P


sharpness = 20.0
LOG2E = math.log2(math.e)
LN2 = math.log(2.0)
LANES = 128


VMEM = pl.BlockSpec(memory_space=pltpu.VMEM)


def params(mib):
    return pltpu.CompilerParams(vmem_limit_bytes=mib << 20)


def unit_rows(values):
    wide = values.astype(jnp.float32)
    scaled = wide * lax.rsqrt(jnp.sum(wide * wide, axis=-1, keepdims=True) + 1e-06)
    return scaled.astype(jnp.bfloat16)


def inner(rows, columns):
    return lax.dot_general(
        rows, columns, (((1,), (1,)), ((), ())), preferred_element_type=jnp.float32
    )


def unit_kernel(values_ref, unit_ref):
    unit_ref[...] = unit_rows(values_ref[...])


def unit_call(values):
    return pl.pallas_call(
        unit_kernel,
        out_shape=jax.ShapeDtypeStruct(values.shape, jnp.bfloat16),
        in_specs=[VMEM],
        out_specs=VMEM,
        compiler_params=params(16),
        name="unit",
        cost_estimate=pl.CostEstimate(
            flops=4 * values.size, bytes_accessed=4 * values.size, transcendentals=values.shape[0]
        ),
    )(values)


def bank_kernel(count, tile, *refs):
    blocks, gallery_ref, earlier, total_ref = (
        refs[:count],
        refs[count],
        refs[count + 1 : -1],
        refs[-1],
    )
    units = [unit_rows(block[...]) for block in blocks]
    unit = jnp.concatenate(units, axis=0) if count > 1 else units[0]
    for start in range(0, gallery_ref.shape[0], tile):
        scores = inner(unit, gallery_ref[start : start + tile, :])
        total = jnp.sum(jnp.exp2(scores * (sharpness * LOG2E)), axis=0, keepdims=True)
        for other in earlier:
            total = total + other[:, start : start + tile]
        total_ref[:, start : start + tile] = total


def bank_call(blocks, gallery_unit, earlier=()):
    columns, depth = gallery_unit.shape
    rows = sum(block.shape[0] for block in blocks)
    tile = math.gcd(columns, 256)
    return pl.pallas_call(
        functools.partial(bank_kernel, len(blocks), tile),
        out_shape=jax.ShapeDtypeStruct((1, columns), jnp.float32),
        in_specs=[VMEM] * (len(blocks) + 1 + len(earlier)),
        out_specs=VMEM,
        compiler_params=params(16),
        name="bank",
        cost_estimate=pl.CostEstimate(
            flops=2 * rows * columns * depth,
            bytes_accessed=2 * depth * (rows + columns),
            transcendentals=rows * columns,
        ),
    )(*blocks, gallery_unit, *earlier)


def test_kernel(count, tile, *refs):
    blocks, gallery_ref, score_ref = refs[:count], refs[count], refs[-1]
    units = [unit_rows(block[...]) for block in blocks]
    unit = jnp.concatenate(units, axis=0) if count > 1 else units[0]
    for start in range(0, gallery_ref.shape[0], tile):
        scores = inner(unit, gallery_ref[start : start + tile, :])
        score_ref[:, start : start + tile] = scores * (sharpness * LOG2E)


def test_call(blocks, gallery_unit):
    columns, depth = gallery_unit.shape
    rows = sum(block.shape[0] for block in blocks)
    tile = math.gcd(columns, 256)
    return pl.pallas_call(
        functools.partial(test_kernel, len(blocks), tile),
        out_shape=jax.ShapeDtypeStruct((rows, columns), jnp.float32),
        in_specs=[VMEM] * (len(blocks) + 1),
        out_specs=VMEM,
        compiler_params=params(16),
        name="test",
        cost_estimate=pl.CostEstimate(
            flops=2 * rows * columns * depth,
            bytes_accessed=2 * depth * (rows + columns) + 4 * rows * columns,
            transcendentals=0,
        ),
    )(*blocks, gallery_unit)


def row_kernel(groups, count, *refs):
    totals, scores, (log_ref, norm_ref, rows_ref) = (
        refs[:groups],
        refs[groups : groups + count],
        refs[-3:],
    )
    total = totals[0][...]
    for other in totals[1:]:
        total = total + other[...]
    log_ref[...] = jnp.log2(total)
    norm_ref[...] = jnp.log(total)
    width = rows_ref.shape[1]
    columns = log_ref.shape[1]
    place = 0
    for score_ref in scores:
        for first in range(0, score_ref.shape[0], width):
            running = jnp.zeros((width, LANES), jnp.float32)
            for start in range(0, columns, LANES):
                piece = score_ref[first : first + width, start : start + LANES]
                running = running + jnp.exp2(piece - log_ref[:, start : start + LANES])
            rows_ref[place : place + 1, :] = jnp.sum(running.T, axis=0, keepdims=True)
            place += 1


def row_call(totals, scores, width):
    columns = scores[0].shape[1]
    rows = sum(score.shape[0] for score in scores)
    return pl.pallas_call(
        functools.partial(row_kernel, len(totals), len(scores)),
        out_shape=(
            jax.ShapeDtypeStruct((1, columns), jnp.float32),
            jax.ShapeDtypeStruct((1, columns), jnp.float32),
            jax.ShapeDtypeStruct((rows // width, width), jnp.float32),
        ),
        in_specs=[VMEM] * (len(totals) + len(scores)),
        out_specs=(VMEM, VMEM, VMEM),
        compiler_params=params(16),
        name="rows",
        cost_estimate=pl.CostEstimate(
            flops=3 * rows * columns,
            bytes_accessed=4 * rows * columns,
            transcendentals=rows * columns,
        ),
    )(*totals, *scores)


def out_kernel(orders, count, split, place_ref, *refs):
    parts, scores, (log_ref, out_ref) = (
        refs[: len(orders)],
        refs[len(orders) : len(orders) + count],
        refs[-2:],
    )
    step = pl.program_id(0)
    height = out_ref.shape[0]
    width = parts[0].shape[1]
    line = height // width
    for block in range(len(orders)):

        @pl.when(step == block)
        def _(block=block):
            for sub in range(line):
                total = None
                for part, order in zip(parts, orders):
                    at = order[block] * line + sub
                    row = part[at : at + 1, :]
                    total = row if total is None else total + row
                wide = jnp.broadcast_to(jnp.log2(total), (LANES, width)).T
                source = scores[block // split]
                first = block % split * height + sub * width
                for start in range(0, log_ref.shape[1], LANES):
                    cut = slice(start, start + LANES)
                    value = source[first : first + width, cut] - log_ref[:, cut] - wide
                    out_ref[sub * width : (sub + 1) * width, cut] = value * LN2


def out_call(place, parts, orders, scores, log_total):
    columns = log_total.shape[1]
    rows = sum(score.shape[0] for score in scores)
    height = rows // len(orders)
    split = scores[0].shape[0] // height
    return pl.pallas_call(
        functools.partial(out_kernel, orders, len(scores), split),
        out_shape=jax.ShapeDtypeStruct((rows, columns), jnp.float32),
        grid_spec=pltpu.PrefetchScalarGridSpec(
            num_scalar_prefetch=1,
            grid=(len(orders),),
            in_specs=[VMEM] * (len(parts) + len(scores) + 1),
            out_specs=pl.BlockSpec((height, columns), lambda step, place: (place[step], 0)),
        ),
        compiler_params=params(16),
        name="out",
        cost_estimate=pl.CostEstimate(
            flops=3 * rows * columns, bytes_accessed=8 * rows * columns, transcendentals=0
        ),
    )(place, *parts, *scores, log_total)


def after(value, token):
    return lax.optimization_barrier((value, token))[0]


def chunk_sizes(rows):
    if rows % 64:
        return [rows]
    return [rows // 2, rows // 4, rows // 4]


def per_device(gallery, querybank, test_queries):
    bank = querybank[0]
    test = test_queries[0]
    gal = lax.axis_size("gal")
    groups = lax.axis_size("qb")
    core = 2 if gal % 2 == 0 else 1
    pairs = gal // core

    def shift(value, pair, flip):
        moves = [
            (i, (i // core + pair) % pairs * core + (i % core ^ flip)) for i in range(gal)
        ]
        return lax.ppermute(value, "gal", moves)

    sizes = chunk_sizes(bank.shape[0])
    starts = [sum(sizes[:i]) for i in range(len(sizes))]
    chunks = [lax.slice_in_dim(bank, s, s + n, axis=0) for s, n in zip(starts, sizes)]

    crossed = []
    for chunk in chunks:
        crossed.append([shift(chunk, pair, 0) for pair in range(1, pairs)])
    test_crossed = [shift(test, pair, 0) for pair in range(1, pairs)]

    def with_partner(block):
        return [block, shift(block, 0, 1)] if core == 2 else [block]

    near = with_partner(bank)
    near_tests = with_partner(test)
    gallery_unit = unit_call(gallery)
    total = bank_call(near, gallery_unit)
    scores = [test_call(near_tests, after(gallery_unit, total))]
    total = after(total, scores[0])
    for group in crossed:
        for block in group:
            block = after(block, total)
            total = bank_call(with_partner(block), gallery_unit, [total])

    totals = [total] + [
        lax.ppermute(total, "qb", [(i, (i + s) % groups) for i in range(groups)])
        for s in range(1, groups)
    ]
    for block in test_crossed:
        block = after(block, total)
        blocks = with_partner(block)
        scores.append(test_call(blocks, gallery_unit))
    width = math.gcd(test.shape[0], LANES)
    log_total, normalizer, part = row_call(totals, scores, width)

    origins = [(pair, flip) for pair in range(pairs) for flip in range(core)]
    parts = [part if pair + flip == 0 else shift(part, pair, flip) for pair, flip in origins]
    orders = [
        [origins.index(((p - pair) % pairs, f ^ flip)) for p, f in origins]
        for pair, flip in origins
    ]

    me = lax.axis_index("gal")
    place = jnp.stack(
        [(me // core - p) % pairs * core + (me % core ^ f) for p, f in origins]
    ).astype(jnp.int32)
    logprob = out_call(place, parts, orders, scores, log_total)
    return (logprob, normalizer.reshape(-1))


def solution(mesh):
    placed = (
        P(("slab", "gal"), None),
        P(("slab", "qb"), "gal", None),
        P(("slab", "qb"), "gal", None),
    )

    return jax.shard_map(
        per_device,
        mesh=mesh,
        in_specs=placed,
        out_specs=(P(("slab", "qb"), "gal"), P(("slab", "gal"))),
        check_vma=False,
    )
```

```python
import functools
import math

import jax
import jax.numpy as jnp
from jax import lax
from jax.experimental import pallas as pl
from jax.experimental.pallas import tpu as pltpu
from jax.sharding import PartitionSpec as P


sharpness = 20.0
LOG2E = math.log2(math.e)
LANES = 128


VMEM = pl.BlockSpec(memory_space=pltpu.VMEM)


def params(mib):
    return pltpu.CompilerParams(vmem_limit_bytes=mib << 20)


def unit_rows(values):
    wide = values.astype(jnp.float32)
    scaled = wide * lax.rsqrt(jnp.sum(wide * wide, axis=-1, keepdims=True) + 1e-06)
    return scaled.astype(jnp.bfloat16)


def inner(rows, columns):
    return lax.dot_general(
        rows, columns, (((1,), (1,)), ((), ())), preferred_element_type=jnp.float32
    )


def unit_kernel(values_ref, unit_ref):
    unit_ref[...] = unit_rows(values_ref[...])


def unit_call(values):
    return pl.pallas_call(
        unit_kernel,
        out_shape=jax.ShapeDtypeStruct(values.shape, jnp.bfloat16),
        in_specs=[VMEM],
        out_specs=VMEM,
        compiler_params=params(16),
        name="unit",
        cost_estimate=pl.CostEstimate(
            flops=4 * values.size, bytes_accessed=4 * values.size, transcendentals=values.shape[0]
        ),
    )(values)


def bank_kernel(count, tile, *refs):
    blocks, gallery_ref, earlier, total_ref = (
        refs[:count],
        refs[count],
        refs[count + 1 : -1],
        refs[-1],
    )
    units = [unit_rows(block[...]) for block in blocks]
    unit = jnp.concatenate(units, axis=0) if count > 1 else units[0]
    for start in range(0, gallery_ref.shape[0], tile):
        scores = inner(unit, gallery_ref[start : start + tile, :])
        total = jnp.sum(jnp.exp2(scores * (sharpness * LOG2E)), axis=0, keepdims=True)
        for other in earlier:
            total = total + other[:, start : start + tile]
        total_ref[:, start : start + tile] = total


def bank_call(blocks, gallery_unit, earlier=()):
    columns, depth = gallery_unit.shape
    rows = sum(block.shape[0] for block in blocks)
    tile = math.gcd(columns, 256)
    return pl.pallas_call(
        functools.partial(bank_kernel, len(blocks), tile),
        out_shape=jax.ShapeDtypeStruct((1, columns), jnp.float32),
        in_specs=[VMEM] * (len(blocks) + 1 + len(earlier)),
        out_specs=VMEM,
        compiler_params=params(16),
        name="bank",
        cost_estimate=pl.CostEstimate(
            flops=2 * rows * columns * depth,
            bytes_accessed=2 * depth * (rows + columns),
            transcendentals=rows * columns,
        ),
    )(*blocks, gallery_unit, *earlier)


def test_kernel(count, tile, *refs):
    blocks, gallery_ref, (score_ref, power_ref) = refs[:count], refs[count], refs[-2:]
    units = [unit_rows(block[...]) for block in blocks]
    unit = jnp.concatenate(units, axis=0) if count > 1 else units[0]
    for start in range(0, gallery_ref.shape[0], tile):
        scores = inner(unit, gallery_ref[start : start + tile, :])
        score_ref[:, start : start + tile] = scores * sharpness
        power_ref[:, start : start + tile] = jnp.exp2(scores * (sharpness * LOG2E))


def test_call(blocks, gallery_unit):
    columns, depth = gallery_unit.shape
    rows = sum(block.shape[0] for block in blocks)
    tile = math.gcd(columns, 256)
    shape = jax.ShapeDtypeStruct((rows, columns), jnp.float32)
    return pl.pallas_call(
        functools.partial(test_kernel, len(blocks), tile),
        out_shape=(shape, shape),
        in_specs=[VMEM] * (len(blocks) + 1),
        out_specs=(VMEM, VMEM),
        compiler_params=params(16),
        name="test",
        cost_estimate=pl.CostEstimate(
            flops=2 * rows * columns * depth,
            bytes_accessed=2 * depth * (rows + columns) + 8 * rows * columns,
            transcendentals=rows * columns,
        ),
    )(*blocks, gallery_unit)


def keep_kernel(total_ref, kept_ref):
    kept_ref[...] = total_ref[...]


def keep_call(total):
    return pl.pallas_call(
        keep_kernel,
        out_shape=jax.ShapeDtypeStruct(total.shape, total.dtype),
        in_specs=[VMEM],
        out_specs=VMEM,
        compiler_params=params(16),
        name="keep",
        cost_estimate=pl.CostEstimate(
            flops=total.size, bytes_accessed=8 * total.size, transcendentals=0
        ),
    )(total)


def row_kernel(groups, *refs):
    totals, powers, (total_ref, rows_ref, inverse_ref) = (
        refs[:groups],
        refs[groups:-3],
        refs[-3:],
    )
    total = totals[0][...]
    for other in totals[1:]:
        total = total + other[...]
    total_ref[...] = total
    inverse_ref[...] = 1.0 / total
    width = rows_ref.shape[1]
    place = 0
    for power_ref in powers:
        for first in range(0, power_ref.shape[0], width):
            running = jnp.zeros((width, LANES), jnp.float32)
            for start in range(0, total_ref.shape[1], LANES):
                cut = slice(start, start + LANES)
                running = running + power_ref[first : first + width, cut] * inverse_ref[:, cut]
            rows_ref[place : place + 1, :] = jnp.sum(running.T, axis=0, keepdims=True)
            place += 1


def row_call(totals, powers, width):
    columns = powers[0].shape[1]
    rows = sum(power.shape[0] for power in powers)
    return pl.pallas_call(
        functools.partial(row_kernel, len(totals)),
        out_shape=(
            jax.ShapeDtypeStruct((1, columns), jnp.float32),
            jax.ShapeDtypeStruct((rows // width, width), jnp.float32),
        ),
        in_specs=[VMEM] * (len(totals) + len(powers)),
        out_specs=(VMEM, VMEM),
        scratch_shapes=[pltpu.VMEM((1, columns), jnp.float32)],
        compiler_params=params(16),
        name="rows",
        cost_estimate=pl.CostEstimate(
            flops=2 * rows * columns, bytes_accessed=4 * rows * columns, transcendentals=0
        ),
    )(*totals, *powers)


def log_kernel(total_ref, log_ref, again_ref):
    value = jnp.log(total_ref[...])
    log_ref[...] = value
    again_ref[...] = value


def log_call(total):
    shape = jax.ShapeDtypeStruct(total.shape, jnp.float32)
    return pl.pallas_call(
        log_kernel,
        out_shape=(shape, shape),
        in_specs=[VMEM],
        out_specs=(VMEM, VMEM),
        compiler_params=params(16),
        name="logs",
        cost_estimate=pl.CostEstimate(
            flops=total.size, bytes_accessed=12 * total.size, transcendentals=total.size
        ),
    )(total)


def out_kernel(origins, orders, pairs, core, height, *refs):
    count = len(origins)
    parts, scores, (log_ref, out_ref, stage, sems) = (
        refs[:count],
        refs[count:-4],
        refs[-4:],
    )
    width = parts[0].shape[1]
    line = height // width
    step = math.gcd(width, 64)
    where = lax.axis_index("gal")
    pair_at, core_at = lax.div(where, core), lax.rem(where, core)
    rows_of = [(score, first) for score in scores for first in range(0, score.shape[0], height)]
    copies = []
    for block, (pair, flip) in enumerate(origins):
        side = core_at if flip == 0 else 1 - core_at
        place = (lax.rem(pair_at + (pairs - pair), pairs) * core + side) * height
        source, first = rows_of[block]
        for sub in range(0, height, width):
            total = None
            for part, order in zip(parts, orders):
                at = order[block] * line + sub // width
                row = part[at : at + 1, :]
                total = row if total is None else total + row
            wide = jnp.broadcast_to(jnp.log(total), (LANES, width)).T
            for piece in range(0, width, step):
                at = len(copies) * step
                begin = first + sub + piece
                for start in range(0, log_ref.shape[1], LANES):
                    cut = slice(start, start + LANES)
                    value = source[begin : begin + step, cut] - log_ref[:, cut]
                    stage[at : at + step, cut] = value - wide[piece : piece + step, :]
                target = pl.multiple_of(place + (sub + piece), step)
                copies.append(
                    pltpu.make_async_copy(
                        stage.at[pl.ds(at, step)],
                        out_ref.at[pl.ds(target, step)],
                        sems.at[len(copies)],
                    )
                )
                if len(copies) > 1:
                    copies[-2].start()
    copies[-1].start()
    for copy in copies:
        copy.wait()


def out_call(origins, orders, pairs, core, parts, scores, log_total):
    columns = log_total.shape[1]
    rows = sum(score.shape[0] for score in scores)
    height = rows // len(origins)
    step = math.gcd(parts[0].shape[1], 64)
    return pl.pallas_call(
        functools.partial(out_kernel, origins, orders, pairs, core, height),
        out_shape=jax.ShapeDtypeStruct((rows, columns), jnp.float32),
        in_specs=[VMEM] * (len(parts) + len(scores) + 1),
        out_specs=pl.BlockSpec(memory_space=pl.ANY),
        scratch_shapes=[
            pltpu.VMEM((rows, columns), jnp.float32),
            pltpu.SemaphoreType.DMA((rows // step,)),
        ],
        compiler_params=params(16),
        name="out",
        cost_estimate=pl.CostEstimate(
            flops=3 * rows * columns, bytes_accessed=8 * rows * columns, transcendentals=0
        ),
    )(*parts, *scores, log_total)


def after(value, token):
    return lax.optimization_barrier((value, token))[0]


def chunk_sizes(rows):
    if rows % 128:
        return [rows]
    first, last = rows // 4, rows // 8
    middle = rows - first - last
    half = (middle // 2 + 15) // 16 * 16
    return [first, half, middle - half, last]


def per_device(gallery, querybank, test_queries):
    bank = querybank[0]
    test = test_queries[0]
    gal = lax.axis_size("gal")
    groups = lax.axis_size("qb")
    core = 2 if gal % 2 == 0 else 1
    pairs = gal // core

    def shift(value, pair, flip):
        moves = [
            (i, (i // core + pair) % pairs * core + (i % core ^ flip)) for i in range(gal)
        ]
        return lax.ppermute(value, "gal", moves)

    sizes = chunk_sizes(bank.shape[0])
    starts = [sum(sizes[:i]) for i in range(len(sizes))]
    chunks = [lax.slice_in_dim(bank, s, s + n, axis=0) for s, n in zip(starts, sizes)]

    crossed = []
    for chunk in chunks:
        crossed += [shift(chunk, pair, 0) for pair in range(1, pairs)]
    test_crossed = [shift(test, pair, 0) for pair in range(1, pairs)]

    near, near_tests = [bank], [test]
    if core == 2:
        near.append(shift(bank, 0, 1))
        near_tests.append(shift(test, 0, 1))
    gallery_unit = unit_call(gallery)
    total = bank_call(near, gallery_unit)
    tables = [test_call(near_tests, after(gallery_unit, total))]
    total = after(total, tables[0][0])

    behind = [total, total]
    for block in crossed:
        blocks = [after(block, behind[-2])]
        if core == 2:
            blocks.append(shift(blocks[0], 0, 1))
        behind.append(bank_call(blocks, gallery_unit, [behind[-1]]))
    total = behind[-1]

    totals = [total]
    for s in range(1, groups):
        totals.append(
            lax.ppermute(total, "qb", [(i, (i + s) % groups) for i in range(groups)])
        )
    totals[0] = keep_call(total)
    for block in test_crossed:
        block = after(block, totals[0])
        blocks = [block]
        if core == 2:
            blocks.append(shift(block, 0, 1))
        for part in blocks:
            tables.append(test_call([part], gallery_unit))
    scores = [score for score, _ in tables]
    width = math.gcd(test.shape[0], LANES)
    total, part = row_call(totals, [power for _, power in tables], width)

    origins = [(pair, flip) for pair in range(pairs) for flip in range(core)]
    parts = [part]
    orders = [list(range(len(origins)))]
    for pair, flip in origins[1:]:
        parts.append(shift(part, pair, flip))
        orders.append(
            [origins.index(((p - pair) % pairs, f ^ flip)) for p, f in origins]
        )
    log_total, normalizer = log_call(total)
    logprob = out_call(origins, orders, pairs, core, parts, scores, log_total)
    return (logprob, normalizer.reshape(-1))


def solution(mesh):
    placed = (
        P(("slab", "gal"), None),
        P(("slab", "qb"), "gal", None),
        P(("slab", "qb"), "gal", None),
    )

    return jax.shard_map(
        per_device,
        mesh=mesh,
        in_specs=placed,
        out_specs=(P(("slab", "qb"), "gal"), P(("slab", "gal"))),
        check_vma=False,
    )
```

```python
import functools
import math

import jax
import jax.numpy as jnp
from jax import lax
from jax.experimental import pallas as pl
from jax.experimental.pallas import tpu as pltpu
from jax.sharding import PartitionSpec as P


sharpness = 20.0
LOG2E = math.log2(math.e)
LANES = 128


VMEM = pl.BlockSpec(memory_space=pltpu.VMEM)


def params(mib):
    return pltpu.CompilerParams(vmem_limit_bytes=mib << 20)


def unit_rows(values):
    wide = values.astype(jnp.float32)
    scaled = wide * lax.rsqrt(jnp.sum(wide * wide, axis=-1, keepdims=True) + 1e-06)
    return scaled.astype(jnp.bfloat16)


def inner(rows, columns):
    return lax.dot_general(
        rows, columns, (((1,), (0,)), ((), ())), preferred_element_type=jnp.float32
    )


def unit_kernel(values_ref, unit_ref):
    step = math.gcd(values_ref.shape[0], 256)
    for start in range(0, values_ref.shape[0], step):
        unit_ref[:, start : start + step] = unit_rows(values_ref[start : start + step, :]).T


def unit_call(values):
    return pl.pallas_call(
        unit_kernel,
        out_shape=jax.ShapeDtypeStruct(values.shape[::-1], jnp.bfloat16),
        in_specs=[VMEM],
        out_specs=VMEM,
        compiler_params=params(16),
        name="unit",
        cost_estimate=pl.CostEstimate(
            flops=4 * values.size, bytes_accessed=4 * values.size, transcendentals=values.shape[0]
        ),
    )(values)


def bank_kernel(count, tile, *refs):
    blocks, gallery_ref, earlier, total_ref = (
        refs[:count],
        refs[count],
        refs[count + 1 : -1],
        refs[-1],
    )
    units = [unit_rows(block[...]) for block in blocks]
    unit = jnp.concatenate(units, axis=0) if count > 1 else units[0]
    for start in range(0, gallery_ref.shape[1], tile):
        scores = inner(unit, gallery_ref[:, start : start + tile])
        total = jnp.sum(jnp.exp2(scores * (sharpness * LOG2E)), axis=0, keepdims=True)
        for other in earlier:
            total = total + other[:, start : start + tile]
        total_ref[:, start : start + tile] = total


def bank_call(blocks, gallery_unit, earlier=()):
    depth, columns = gallery_unit.shape
    rows = sum(block.shape[0] for block in blocks)
    tile = math.gcd(columns, 256)
    return pl.pallas_call(
        functools.partial(bank_kernel, len(blocks), tile),
        out_shape=jax.ShapeDtypeStruct((1, columns), jnp.float32),
        in_specs=[VMEM] * (len(blocks) + 1 + len(earlier)),
        out_specs=VMEM,
        compiler_params=params(16),
        name="bank",
        cost_estimate=pl.CostEstimate(
            flops=2 * rows * columns * depth,
            bytes_accessed=2 * depth * (rows + columns),
            transcendentals=rows * columns,
        ),
    )(*blocks, gallery_unit, *earlier)


def test_kernel(count, tile, *refs):
    blocks, gallery_ref, (score_ref, power_ref) = refs[:count], refs[count], refs[-2:]
    units = [unit_rows(block[...]) for block in blocks]
    unit = jnp.concatenate(units, axis=0) if count > 1 else units[0]
    for start in range(0, gallery_ref.shape[1], tile):
        scores = inner(unit, gallery_ref[:, start : start + tile])
        score_ref[:, start : start + tile] = scores * sharpness
        power_ref[:, start : start + tile] = jnp.exp2(scores * (sharpness * LOG2E))


def test_call(blocks, gallery_unit):
    depth, columns = gallery_unit.shape
    rows = sum(block.shape[0] for block in blocks)
    tile = math.gcd(columns, 256)
    shape = jax.ShapeDtypeStruct((rows, columns), jnp.float32)
    return pl.pallas_call(
        functools.partial(test_kernel, len(blocks), tile),
        out_shape=(shape, shape),
        in_specs=[VMEM] * (len(blocks) + 1),
        out_specs=(VMEM, VMEM),
        compiler_params=params(16),
        name="test",
        cost_estimate=pl.CostEstimate(
            flops=2 * rows * columns * depth,
            bytes_accessed=2 * depth * (rows + columns) + 8 * rows * columns,
            transcendentals=rows * columns,
        ),
    )(*blocks, gallery_unit)


def keep_kernel(total_ref, kept_ref):
    kept_ref[...] = total_ref[...]


def keep_call(total):
    return pl.pallas_call(
        keep_kernel,
        out_shape=jax.ShapeDtypeStruct(total.shape, total.dtype),
        in_specs=[VMEM],
        out_specs=VMEM,
        compiler_params=params(16),
        name="keep",
        cost_estimate=pl.CostEstimate(
            flops=total.size, bytes_accessed=8 * total.size, transcendentals=0
        ),
    )(total)


def row_kernel(groups, *refs):
    totals, powers, (total_ref, rows_ref, inverse_ref) = (
        refs[:groups],
        refs[groups:-3],
        refs[-3:],
    )
    total = totals[0][...]
    for other in totals[1:]:
        total = total + other[...]
    total_ref[...] = total
    inverse_ref[...] = 1.0 / total
    width = rows_ref.shape[1]
    place = 0
    for power_ref in powers:
        for first in range(0, power_ref.shape[0], width):
            running = jnp.zeros((width, LANES), jnp.float32)
            for start in range(0, total_ref.shape[1], LANES):
                cut = slice(start, start + LANES)
                running = running + power_ref[first : first + width, cut] * inverse_ref[:, cut]
            rows_ref[place : place + 1, :] = jnp.sum(running.T, axis=0, keepdims=True)
            place += 1


def row_call(totals, powers, width):
    columns = powers[0].shape[1]
    rows = sum(power.shape[0] for power in powers)
    return pl.pallas_call(
        functools.partial(row_kernel, len(totals)),
        out_shape=(
            jax.ShapeDtypeStruct((1, columns), jnp.float32),
            jax.ShapeDtypeStruct((rows // width, width), jnp.float32),
        ),
        in_specs=[VMEM] * (len(totals) + len(powers)),
        out_specs=(VMEM, VMEM),
        scratch_shapes=[pltpu.VMEM((1, columns), jnp.float32)],
        compiler_params=params(16),
        name="rows",
        cost_estimate=pl.CostEstimate(
            flops=2 * rows * columns, bytes_accessed=4 * rows * columns, transcendentals=0
        ),
    )(*totals, *powers)


def log_kernel(total_ref, log_ref, again_ref):
    value = jnp.log(total_ref[...])
    log_ref[...] = value
    again_ref[...] = value


def log_call(total):
    shape = jax.ShapeDtypeStruct(total.shape, jnp.float32)
    return pl.pallas_call(
        log_kernel,
        out_shape=(shape, shape),
        in_specs=[VMEM],
        out_specs=(VMEM, VMEM),
        compiler_params=params(16),
        name="logs",
        cost_estimate=pl.CostEstimate(
            flops=total.size, bytes_accessed=12 * total.size, transcendentals=total.size
        ),
    )(total)


def out_kernel(origins, orders, pairs, core, height, *refs):
    count = len(origins)
    parts, scores, (log_ref, out_ref, stage, sems) = (
        refs[:count],
        refs[count:-4],
        refs[-4:],
    )
    width = parts[0].shape[1]
    line = height // width
    step = math.gcd(width, 64)
    where = lax.axis_index("gal")
    pair_at, core_at = lax.div(where, core), lax.rem(where, core)
    rows_of = [(score, first) for score in scores for first in range(0, score.shape[0], height)]
    copies = []
    for block, (pair, flip) in enumerate(origins):
        side = core_at if flip == 0 else 1 - core_at
        place = (lax.rem(pair_at + (pairs - pair), pairs) * core + side) * height
        source, first = rows_of[block]
        for sub in range(0, height, width):
            total = None
            for part, order in zip(parts, orders):
                at = order[block] * line + sub // width
                row = part[at : at + 1, :]
                total = row if total is None else total + row
            wide = jnp.broadcast_to(jnp.log(total), (LANES, width)).T
            for piece in range(0, width, step):
                at = len(copies) * step
                begin = first + sub + piece
                for start in range(0, log_ref.shape[1], LANES):
                    cut = slice(start, start + LANES)
                    value = source[begin : begin + step, cut] - log_ref[:, cut]
                    stage[at : at + step, cut] = value - wide[piece : piece + step, :]
                target = pl.multiple_of(place + (sub + piece), step)
                copies.append(
                    pltpu.make_async_copy(
                        stage.at[pl.ds(at, step)],
                        out_ref.at[pl.ds(target, step)],
                        sems.at[len(copies)],
                    )
                )
                if len(copies) > 1:
                    copies[-2].start()
    copies[-1].start()
    for copy in copies:
        copy.wait()


def out_call(origins, orders, pairs, core, parts, scores, log_total):
    columns = log_total.shape[1]
    rows = sum(score.shape[0] for score in scores)
    height = rows // len(origins)
    step = math.gcd(parts[0].shape[1], 64)
    return pl.pallas_call(
        functools.partial(out_kernel, origins, orders, pairs, core, height),
        out_shape=jax.ShapeDtypeStruct((rows, columns), jnp.float32),
        in_specs=[VMEM] * (len(parts) + len(scores) + 1),
        out_specs=pl.BlockSpec(memory_space=pl.ANY),
        scratch_shapes=[
            pltpu.VMEM((rows, columns), jnp.float32),
            pltpu.SemaphoreType.DMA((rows // step,)),
        ],
        compiler_params=params(16),
        name="out",
        cost_estimate=pl.CostEstimate(
            flops=3 * rows * columns, bytes_accessed=8 * rows * columns, transcendentals=0
        ),
    )(*parts, *scores, log_total)


def after(value, token):
    return lax.optimization_barrier((value, token))[0]


def chunk_sizes(rows):
    if rows % 128:
        return [rows]
    first, last = rows // 4, rows // 8
    middle = rows - first - last
    half = (middle // 2 + 15) // 16 * 16
    return [first, half, middle - half, last]


def per_device(gallery, querybank, test_queries):
    bank = querybank[0]
    test = test_queries[0]
    gal = lax.axis_size("gal")
    groups = lax.axis_size("qb")
    core = 2 if gal % 2 == 0 else 1
    pairs = gal // core

    def shift(value, pair, flip):
        moves = [
            (i, (i // core + pair) % pairs * core + (i % core ^ flip)) for i in range(gal)
        ]
        return lax.ppermute(value, "gal", moves)

    sizes = chunk_sizes(bank.shape[0])
    starts = [sum(sizes[:i]) for i in range(len(sizes))]
    chunks = [lax.slice_in_dim(bank, s, s + n, axis=0) for s, n in zip(starts, sizes)]

    crossed = []
    for chunk in chunks:
        crossed += [shift(chunk, pair, 0) for pair in range(1, pairs)]
    test_crossed = [shift(test, pair, 0) for pair in range(1, pairs)]

    near, near_tests = [bank], [test]
    if core == 2:
        near.append(shift(bank, 0, 1))
        near_tests.append(shift(test, 0, 1))
    gallery_unit = unit_call(gallery)
    total = bank_call(near, gallery_unit)
    summed = total
    tables = [test_call(near_tests, after(gallery_unit, total))]
    total = after(total, tables[0][0])

    behind = [total]
    for index, block in enumerate(crossed):
        blocks = [after(block, behind[index // 2 * 2] if index > 1 else summed)]
        if core == 2:
            blocks.append(shift(blocks[0], 0, 1))
        behind.append(bank_call(blocks, gallery_unit, [behind[-1]]))
    total = behind[-1]

    totals = [total]
    for s in range(1, groups):
        totals.append(
            lax.ppermute(total, "qb", [(i, (i + s) % groups) for i in range(groups)])
        )
    totals[0] = keep_call(total)
    for block in test_crossed:
        block = after(block, totals[0])
        blocks = [block]
        if core == 2:
            blocks.append(shift(block, 0, 1))
        for part in blocks:
            tables.append(test_call([part], gallery_unit))
    scores = [score for score, _ in tables]
    width = math.gcd(test.shape[0], LANES)
    total, part = row_call(totals, [power for _, power in tables], width)

    origins = [(pair, flip) for pair in range(pairs) for flip in range(core)]
    parts = [part]
    orders = [list(range(len(origins)))]
    for pair, flip in origins[1:]:
        parts.append(shift(part, pair, flip))
        orders.append(
            [origins.index(((p - pair) % pairs, f ^ flip)) for p, f in origins]
        )
    log_total, normalizer = log_call(total)
    logprob = out_call(origins, orders, pairs, core, parts, scores, log_total)
    return (logprob, normalizer.reshape(-1))


def solution(mesh):
    placed = (
        P(("slab", "gal"), None),
        P(("slab", "qb"), "gal", None),
        P(("slab", "qb"), "gal", None),
    )

    return jax.shard_map(
        per_device,
        mesh=mesh,
        in_specs=placed,
        out_specs=(P(("slab", "qb"), "gal"), P(("slab", "gal"))),
        check_vma=False,
    )
```

```python
import functools
import math

import jax
import jax.numpy as jnp
from jax import lax
from jax.experimental import pallas as pl
from jax.experimental.pallas import tpu as pltpu
from jax.sharding import PartitionSpec as P


sharpness = 20.0
LOG2E = math.log2(math.e)
LANES = 128


VMEM = pl.BlockSpec(memory_space=pltpu.VMEM)


def params(mib):
    return pltpu.CompilerParams(vmem_limit_bytes=mib << 20)


def unit_rows(values):
    wide = values.astype(jnp.float32)
    scaled = wide * lax.rsqrt(jnp.sum(wide * wide, axis=-1, keepdims=True) + 1e-06)
    return scaled.astype(jnp.bfloat16)


def inner(rows, columns):
    return lax.dot_general(
        rows, columns, (((1,), (0,)), ((), ())), preferred_element_type=jnp.float32
    )


def cut_kernel(starts, source_ref, *refs):
    outs, sems = refs[:-1], refs[-1]
    copies = [
        pltpu.make_async_copy(source_ref.at[pl.ds(start, out.shape[0])], out, sems.at[index])
        for index, (start, out) in enumerate(zip(starts, outs))
    ]
    for copy in copies:
        copy.start()
    for copy in copies:
        copy.wait()


def cut_call(source, starts, sizes):
    shapes = [jax.ShapeDtypeStruct((size, source.shape[1]), source.dtype) for size in sizes]
    return pl.pallas_call(
        functools.partial(cut_kernel, starts),
        out_shape=shapes,
        in_specs=[pl.BlockSpec(memory_space=pltpu.HBM)],
        out_specs=[VMEM] * len(sizes),
        scratch_shapes=[pltpu.SemaphoreType.DMA((len(sizes),))],
        compiler_params=params(4),
        name="cut",
        cost_estimate=pl.CostEstimate(
            flops=0, bytes_accessed=4 * sum(sizes) * source.shape[1], transcendentals=0
        ),
    )(source)


def unit_kernel(step, values_ref, unit_ref, stage, sems):
    rows = values_ref.shape[0]
    copies = [
        pltpu.make_async_copy(
            values_ref.at[pl.ds(start, step)], stage.at[pl.ds(start, step)], sems.at[start // step]
        )
        for start in range(0, rows, step)
    ]
    ahead = 3
    for copy in copies[:ahead]:
        copy.start()
    for index, start in enumerate(range(0, rows, step)):
        copies[index].wait()
        if index + ahead < len(copies):
            copies[index + ahead].start()
        unit_ref[:, start : start + step] = unit_rows(stage[start : start + step, :]).T


def unit_call(values):
    step = math.gcd(values.shape[0], 256)
    return pl.pallas_call(
        functools.partial(unit_kernel, step),
        out_shape=jax.ShapeDtypeStruct(values.shape[::-1], jnp.bfloat16),
        in_specs=[pl.BlockSpec(memory_space=pltpu.HBM)],
        out_specs=VMEM,
        scratch_shapes=[
            pltpu.VMEM(values.shape, values.dtype),
            pltpu.SemaphoreType.DMA((values.shape[0] // step,)),
        ],
        compiler_params=params(16),
        name="unit",
        cost_estimate=pl.CostEstimate(
            flops=4 * values.size, bytes_accessed=4 * values.size, transcendentals=values.shape[0]
        ),
    )(pltpu.with_memory_space_constraint(values, pltpu.HBM))


def bank_kernel(count, tile, *refs):
    blocks, gallery_ref, earlier, total_ref = (
        refs[:count],
        refs[count],
        refs[count + 1 : -1],
        refs[-1],
    )
    units = [unit_rows(block[...]) for block in blocks]
    unit = jnp.concatenate(units, axis=0) if count > 1 else units[0]
    for start in range(0, gallery_ref.shape[1], tile):
        scores = inner(unit, gallery_ref[:, start : start + tile])
        total = jnp.sum(jnp.exp2(scores * (sharpness * LOG2E)), axis=0, keepdims=True)
        for other in earlier:
            total = total + other[:, start : start + tile]
        total_ref[:, start : start + tile] = total


def bank_call(blocks, gallery_unit, earlier=()):
    depth, columns = gallery_unit.shape
    rows = sum(block.shape[0] for block in blocks)
    tile = math.gcd(columns, 256)
    return pl.pallas_call(
        functools.partial(bank_kernel, len(blocks), tile),
        out_shape=jax.ShapeDtypeStruct((1, columns), jnp.float32),
        in_specs=[VMEM] * (len(blocks) + 1 + len(earlier)),
        out_specs=VMEM,
        compiler_params=params(16),
        name="bank",
        cost_estimate=pl.CostEstimate(
            flops=2 * rows * columns * depth,
            bytes_accessed=2 * depth * (rows + columns),
            transcendentals=rows * columns,
        ),
    )(*blocks, gallery_unit, *earlier)


def test_kernel(count, tile, *refs):
    blocks, gallery_ref, (score_ref, power_ref) = refs[:count], refs[count], refs[-2:]
    units = [unit_rows(block[...]) for block in blocks]
    unit = jnp.concatenate(units, axis=0) if count > 1 else units[0]
    for start in range(0, gallery_ref.shape[1], tile):
        scores = inner(unit, gallery_ref[:, start : start + tile])
        score_ref[:, start : start + tile] = scores * sharpness
        power_ref[:, start : start + tile] = jnp.exp2(scores * (sharpness * LOG2E))


def test_call(blocks, gallery_unit):
    depth, columns = gallery_unit.shape
    rows = sum(block.shape[0] for block in blocks)
    tile = math.gcd(columns, 256)
    shape = jax.ShapeDtypeStruct((rows, columns), jnp.float32)
    return pl.pallas_call(
        functools.partial(test_kernel, len(blocks), tile),
        out_shape=(shape, shape),
        in_specs=[VMEM] * (len(blocks) + 1),
        out_specs=(VMEM, VMEM),
        compiler_params=params(16),
        name="test",
        cost_estimate=pl.CostEstimate(
            flops=2 * rows * columns * depth,
            bytes_accessed=2 * depth * (rows + columns) + 8 * rows * columns,
            transcendentals=rows * columns,
        ),
    )(*blocks, gallery_unit)


def keep_kernel(total_ref, kept_ref):
    kept_ref[...] = total_ref[...]


def keep_call(total):
    return pl.pallas_call(
        keep_kernel,
        out_shape=jax.ShapeDtypeStruct(total.shape, total.dtype),
        in_specs=[VMEM],
        out_specs=VMEM,
        compiler_params=params(16),
        name="keep",
        cost_estimate=pl.CostEstimate(
            flops=total.size, bytes_accessed=8 * total.size, transcendentals=0
        ),
    )(total)


def row_kernel(groups, *refs):
    totals, powers, (total_ref, rows_ref, inverse_ref) = (
        refs[:groups],
        refs[groups:-3],
        refs[-3:],
    )
    total = totals[0][...]
    for other in totals[1:]:
        total = total + other[...]
    total_ref[...] = total
    inverse_ref[...] = 1.0 / total
    width = rows_ref.shape[1]
    place = 0
    for power_ref in powers:
        for first in range(0, power_ref.shape[0], width):
            running = jnp.zeros((width, LANES), jnp.float32)
            for start in range(0, total_ref.shape[1], LANES):
                cut = slice(start, start + LANES)
                running = running + power_ref[first : first + width, cut] * inverse_ref[:, cut]
            rows_ref[place : place + 1, :] = jnp.sum(running.T, axis=0, keepdims=True)
            place += 1


def row_call(totals, powers, width):
    columns = powers[0].shape[1]
    rows = sum(power.shape[0] for power in powers)
    return pl.pallas_call(
        functools.partial(row_kernel, len(totals)),
        out_shape=(
            jax.ShapeDtypeStruct((1, columns), jnp.float32),
            jax.ShapeDtypeStruct((rows // width, width), jnp.float32),
        ),
        in_specs=[VMEM] * (len(totals) + len(powers)),
        out_specs=(VMEM, VMEM),
        scratch_shapes=[pltpu.VMEM((1, columns), jnp.float32)],
        compiler_params=params(16),
        name="rows",
        cost_estimate=pl.CostEstimate(
            flops=2 * rows * columns, bytes_accessed=4 * rows * columns, transcendentals=0
        ),
    )(*totals, *powers)


def log_kernel(total_ref, log_ref, again_ref):
    value = jnp.log(total_ref[...])
    log_ref[...] = value
    again_ref[...] = value


def log_call(total):
    shape = jax.ShapeDtypeStruct(total.shape, jnp.float32)
    return pl.pallas_call(
        log_kernel,
        out_shape=(shape, shape),
        in_specs=[VMEM],
        out_specs=(VMEM, VMEM),
        compiler_params=params(16),
        name="logs",
        cost_estimate=pl.CostEstimate(
            flops=total.size, bytes_accessed=12 * total.size, transcendentals=total.size
        ),
    )(total)


def out_kernel(origins, orders, pairs, core, height, *refs):
    count = len(origins)
    parts, scores, (log_ref, out_ref, stage, sems) = (
        refs[:count],
        refs[count:-4],
        refs[-4:],
    )
    width = parts[0].shape[1]
    line = height // width
    step = math.gcd(width, 64)
    where = lax.axis_index("gal")
    pair_at, core_at = lax.div(where, core), lax.rem(where, core)
    rows_of = [(score, first) for score in scores for first in range(0, score.shape[0], height)]
    copies = []
    for block, (pair, flip) in enumerate(origins):
        side = core_at if flip == 0 else 1 - core_at
        place = (lax.rem(pair_at + (pairs - pair), pairs) * core + side) * height
        source, first = rows_of[block]
        for sub in range(0, height, width):
            total = None
            for part, order in zip(parts, orders):
                at = order[block] * line + sub // width
                row = part[at : at + 1, :]
                total = row if total is None else total + row
            wide = jnp.broadcast_to(jnp.log(total), (LANES, width)).T
            for piece in range(0, width, step):
                at = len(copies) * step
                begin = first + sub + piece
                for start in range(0, log_ref.shape[1], LANES):
                    cut = slice(start, start + LANES)
                    value = source[begin : begin + step, cut] - log_ref[:, cut]
                    stage[at : at + step, cut] = value - wide[piece : piece + step, :]
                target = pl.multiple_of(place + (sub + piece), step)
                copies.append(
                    pltpu.make_async_copy(
                        stage.at[pl.ds(at, step)],
                        out_ref.at[pl.ds(target, step)],
                        sems.at[len(copies)],
                    )
                )
                if len(copies) > 1:
                    copies[-2].start()
    copies[-1].start()
    for copy in copies:
        copy.wait()


def out_call(origins, orders, pairs, core, parts, scores, log_total):
    columns = log_total.shape[1]
    rows = sum(score.shape[0] for score in scores)
    height = rows // len(origins)
    step = math.gcd(parts[0].shape[1], 64)
    return pl.pallas_call(
        functools.partial(out_kernel, origins, orders, pairs, core, height),
        out_shape=jax.ShapeDtypeStruct((rows, columns), jnp.float32),
        in_specs=[VMEM] * (len(parts) + len(scores) + 1),
        out_specs=pl.BlockSpec(memory_space=pl.ANY),
        scratch_shapes=[
            pltpu.VMEM((rows, columns), jnp.float32),
            pltpu.SemaphoreType.DMA((rows // step,)),
        ],
        compiler_params=params(16),
        name="out",
        cost_estimate=pl.CostEstimate(
            flops=3 * rows * columns, bytes_accessed=8 * rows * columns, transcendentals=0
        ),
    )(*parts, *scores, log_total)


def after(value, token):
    return lax.optimization_barrier((value, token))[0]


def chunk_sizes(rows):
    if rows % 128:
        return [rows]
    return [rows * part // 32 for part in (8, 12, 8, 4)]


def per_device(gallery, querybank, test_queries):
    bank = querybank[0]
    test = test_queries[0]
    gal = lax.axis_size("gal")
    groups = lax.axis_size("qb")
    core = 2 if gal % 2 == 0 else 1
    pairs = gal // core

    def shift(value, pair, flip):
        moves = [
            (i, (i // core + pair) % pairs * core + (i % core ^ flip)) for i in range(gal)
        ]
        return lax.ppermute(value, "gal", moves)

    sizes = chunk_sizes(bank.shape[0])
    starts = [sum(sizes[:i]) for i in range(len(sizes))]
    chunks = cut_call(bank, starts[:1], sizes[:1])
    if len(sizes) > 1:
        chunks += cut_call(bank, starts[1:], sizes[1:])

    crossed = []
    for chunk in chunks:
        crossed += [shift(chunk, pair, 0) for pair in range(1, pairs)]
    test_crossed = [shift(test, pair, 0) for pair in range(1, pairs)]

    near, near_tests = [*chunks], [test]
    if core == 2:
        near.append(shift(bank, 0, 1))
        near_tests.append(shift(test, 0, 1))
    gallery_unit = unit_call(gallery)
    total = bank_call(near, gallery_unit)
    summed = total
    tables = [test_call(near_tests, after(gallery_unit, total))]
    total = after(total, tables[0][0])

    behind = [total]
    for index, block in enumerate(crossed):
        blocks = [after(block, behind[index // 2 * 2] if index else summed)]
        if core == 2:
            blocks.append(shift(blocks[0], 0, 1))
        behind.append(bank_call(blocks, gallery_unit, [behind[-1]]))
    total = behind[-1]

    totals = [total]
    for s in range(1, groups):
        totals.append(
            lax.ppermute(total, "qb", [(i, (i + s) % groups) for i in range(groups)])
        )
    totals[0] = keep_call(total)
    for block in test_crossed:
        block = after(block, totals[0])
        blocks = [block]
        if core == 2:
            blocks.append(shift(block, 0, 1))
        for part in blocks:
            tables.append(test_call([part], gallery_unit))
    scores = [score for score, _ in tables]
    width = math.gcd(test.shape[0], LANES)
    total, part = row_call(totals, [power for _, power in tables], width)

    origins = [(pair, flip) for pair in range(pairs) for flip in range(core)]
    parts = [part]
    orders = [list(range(len(origins)))]
    for pair, flip in origins[1:]:
        parts.append(shift(part, pair, flip))
        orders.append(
            [origins.index(((p - pair) % pairs, f ^ flip)) for p, f in origins]
        )
    log_total, normalizer = log_call(total)
    logprob = out_call(origins, orders, pairs, core, parts, scores, log_total)
    return (logprob, normalizer.reshape(-1))


def solution(mesh):
    placed = (
        P(("slab", "gal"), None),
        P(("slab", "qb"), "gal", None),
        P(("slab", "qb"), "gal", None),
    )

    return jax.shard_map(
        per_device,
        mesh=mesh,
        in_specs=placed,
        out_specs=(P(("slab", "qb"), "gal"), P(("slab", "gal"))),
        check_vma=False,
    )
```

```python
import functools
import math

import jax
import jax.numpy as jnp
from jax import lax
from jax.experimental import pallas as pl
from jax.experimental.pallas import tpu as pltpu
from jax.sharding import PartitionSpec as P


sharpness = 20.0
LOG2E = math.log2(math.e)
LANES = 128


VMEM = pl.BlockSpec(memory_space=pltpu.VMEM)


def params(mib):
    return pltpu.CompilerParams(vmem_limit_bytes=mib << 20)


def unit_rows(values):
    wide = values.astype(jnp.float32)
    scaled = wide * lax.rsqrt(jnp.sum(wide * wide, axis=-1, keepdims=True) + 1e-06)
    return scaled.astype(jnp.bfloat16)


def inner(rows, columns):
    return lax.dot_general(
        rows, columns, (((1,), (0,)), ((), ())), preferred_element_type=jnp.float32
    )


def cut_kernel(starts, source_ref, *refs):
    outs, sems = refs[:-1], refs[-1]
    copies = [
        pltpu.make_async_copy(source_ref.at[pl.ds(start, out.shape[0])], out, sems.at[index])
        for index, (start, out) in enumerate(zip(starts, outs))
    ]
    for copy in copies:
        copy.start()
    for copy in copies:
        copy.wait()


def cut_call(source, starts, sizes):
    shapes = [jax.ShapeDtypeStruct((size, source.shape[1]), source.dtype) for size in sizes]
    return pl.pallas_call(
        functools.partial(cut_kernel, starts),
        out_shape=shapes,
        in_specs=[pl.BlockSpec(memory_space=pltpu.HBM)],
        out_specs=[VMEM] * len(sizes),
        scratch_shapes=[pltpu.SemaphoreType.DMA((len(sizes),))],
        compiler_params=params(4),
        name="cut",
        cost_estimate=pl.CostEstimate(
            flops=0, bytes_accessed=4 * sum(sizes) * source.shape[1], transcendentals=0
        ),
    )(source)


def unit_kernel(step, values_ref, unit_ref, stage, sems):
    rows = values_ref.shape[0]
    copies = [
        pltpu.make_async_copy(
            values_ref.at[pl.ds(start, step)], stage.at[pl.ds(start, step)], sems.at[start // step]
        )
        for start in range(0, rows, step)
    ]
    for copy in copies:
        copy.start()
    for start, copy in zip(range(0, rows, step), copies):
        copy.wait()
        unit_ref[:, start : start + step] = unit_rows(stage[start : start + step, :]).T


def unit_call(values):
    step = math.gcd(values.shape[0], 512)
    return pl.pallas_call(
        functools.partial(unit_kernel, step),
        out_shape=jax.ShapeDtypeStruct(values.shape[::-1], jnp.bfloat16),
        in_specs=[pl.BlockSpec(memory_space=pltpu.HBM)],
        out_specs=VMEM,
        scratch_shapes=[
            pltpu.VMEM(values.shape, values.dtype),
            pltpu.SemaphoreType.DMA((values.shape[0] // step,)),
        ],
        compiler_params=params(16),
        name="unit",
        cost_estimate=pl.CostEstimate(
            flops=4 * values.size, bytes_accessed=4 * values.size, transcendentals=values.shape[0]
        ),
    )(pltpu.with_memory_space_constraint(values, pltpu.HBM))


def bank_kernel(count, tile, *refs):
    blocks, gallery_ref, earlier, total_ref = (
        refs[:count],
        refs[count],
        refs[count + 1 : -1],
        refs[-1],
    )
    units = [unit_rows(block[...]) for block in blocks]
    unit = jnp.concatenate(units, axis=0) if count > 1 else units[0]
    for start in range(0, gallery_ref.shape[1], tile):
        scores = inner(unit, gallery_ref[:, start : start + tile])
        total = jnp.sum(jnp.exp2(scores * (sharpness * LOG2E)), axis=0, keepdims=True)
        for other in earlier:
            total = total + other[:, start : start + tile]
        total_ref[:, start : start + tile] = total


def bank_call(blocks, gallery_unit, earlier=()):
    depth, columns = gallery_unit.shape
    rows = sum(block.shape[0] for block in blocks)
    tile = math.gcd(columns, 256)
    return pl.pallas_call(
        functools.partial(bank_kernel, len(blocks), tile),
        out_shape=jax.ShapeDtypeStruct((1, columns), jnp.float32),
        in_specs=[VMEM] * (len(blocks) + 1 + len(earlier)),
        out_specs=VMEM,
        compiler_params=params(16),
        name="bank",
        cost_estimate=pl.CostEstimate(
            flops=2 * rows * columns * depth,
            bytes_accessed=2 * depth * (rows + columns),
            transcendentals=rows * columns,
        ),
    )(*blocks, gallery_unit, *earlier)


def test_kernel(count, tile, *refs):
    blocks, gallery_ref, (score_ref, power_ref) = refs[:count], refs[count], refs[-2:]
    units = [unit_rows(block[...]) for block in blocks]
    unit = jnp.concatenate(units, axis=0) if count > 1 else units[0]
    for start in range(0, gallery_ref.shape[1], tile):
        scores = inner(unit, gallery_ref[:, start : start + tile])
        score_ref[:, start : start + tile] = scores * sharpness
        power_ref[:, start : start + tile] = jnp.exp2(scores * (sharpness * LOG2E))


def test_call(blocks, gallery_unit):
    depth, columns = gallery_unit.shape
    rows = sum(block.shape[0] for block in blocks)
    tile = math.gcd(columns, 256)
    shape = jax.ShapeDtypeStruct((rows, columns), jnp.float32)
    return pl.pallas_call(
        functools.partial(test_kernel, len(blocks), tile),
        out_shape=(shape, shape),
        in_specs=[VMEM] * (len(blocks) + 1),
        out_specs=(VMEM, VMEM),
        compiler_params=params(16),
        name="test",
        cost_estimate=pl.CostEstimate(
            flops=2 * rows * columns * depth,
            bytes_accessed=2 * depth * (rows + columns) + 8 * rows * columns,
            transcendentals=rows * columns,
        ),
    )(*blocks, gallery_unit)


def keep_kernel(total_ref, kept_ref):
    kept_ref[...] = total_ref[...]


def keep_call(total):
    return pl.pallas_call(
        keep_kernel,
        out_shape=jax.ShapeDtypeStruct(total.shape, total.dtype),
        in_specs=[VMEM],
        out_specs=VMEM,
        compiler_params=params(16),
        name="keep",
        cost_estimate=pl.CostEstimate(
            flops=total.size, bytes_accessed=8 * total.size, transcendentals=0
        ),
    )(total)


def row_kernel(groups, *refs):
    totals, powers, (total_ref, rows_ref, inverse_ref) = (
        refs[:groups],
        refs[groups:-3],
        refs[-3:],
    )
    total = totals[0][...]
    for other in totals[1:]:
        total = total + other[...]
    total_ref[...] = total
    inverse_ref[...] = 1.0 / total
    width = rows_ref.shape[1]
    place = 0
    for power_ref in powers:
        for first in range(0, power_ref.shape[0], width):
            running = jnp.zeros((width, LANES), jnp.float32)
            for start in range(0, total_ref.shape[1], LANES):
                cut = slice(start, start + LANES)
                running = running + power_ref[first : first + width, cut] * inverse_ref[:, cut]
            rows_ref[place : place + 1, :] = jnp.sum(running.T, axis=0, keepdims=True)
            place += 1


def row_call(totals, powers, width):
    columns = powers[0].shape[1]
    rows = sum(power.shape[0] for power in powers)
    return pl.pallas_call(
        functools.partial(row_kernel, len(totals)),
        out_shape=(
            jax.ShapeDtypeStruct((1, columns), jnp.float32),
            jax.ShapeDtypeStruct((rows // width, width), jnp.float32),
        ),
        in_specs=[VMEM] * (len(totals) + len(powers)),
        out_specs=(VMEM, VMEM),
        scratch_shapes=[pltpu.VMEM((1, columns), jnp.float32)],
        compiler_params=params(16),
        name="rows",
        cost_estimate=pl.CostEstimate(
            flops=2 * rows * columns, bytes_accessed=4 * rows * columns, transcendentals=0
        ),
    )(*totals, *powers)


def log_kernel(total_ref, log_ref, again_ref):
    value = jnp.log(total_ref[...])
    log_ref[...] = value
    again_ref[...] = value


def log_call(total):
    shape = jax.ShapeDtypeStruct(total.shape, jnp.float32)
    return pl.pallas_call(
        log_kernel,
        out_shape=(shape, shape),
        in_specs=[VMEM],
        out_specs=(VMEM, VMEM),
        compiler_params=params(16),
        name="logs",
        cost_estimate=pl.CostEstimate(
            flops=total.size, bytes_accessed=12 * total.size, transcendentals=total.size
        ),
    )(total)


def out_kernel(origins, orders, pairs, core, height, *refs):
    count = len(origins)
    parts, scores, (log_ref, out_ref, stage, sems) = (
        refs[:count],
        refs[count:-4],
        refs[-4:],
    )
    width = parts[0].shape[1]
    line = height // width
    step = math.gcd(width, 64)
    where = lax.axis_index("gal")
    pair_at, core_at = lax.div(where, core), lax.rem(where, core)
    rows_of = [(score, first) for score in scores for first in range(0, score.shape[0], height)]
    copies = []
    for block, (pair, flip) in enumerate(origins):
        side = core_at if flip == 0 else 1 - core_at
        place = (lax.rem(pair_at + (pairs - pair), pairs) * core + side) * height
        source, first = rows_of[block]
        for sub in range(0, height, width):
            total = None
            for part, order in zip(parts, orders):
                at = order[block] * line + sub // width
                row = part[at : at + 1, :]
                total = row if total is None else total + row
            wide = jnp.broadcast_to(jnp.log(total), (LANES, width)).T
            for piece in range(0, width, step):
                at = len(copies) * step
                begin = first + sub + piece
                for start in range(0, log_ref.shape[1], LANES):
                    cut = slice(start, start + LANES)
                    value = source[begin : begin + step, cut] - log_ref[:, cut]
                    stage[at : at + step, cut] = value - wide[piece : piece + step, :]
                target = pl.multiple_of(place + (sub + piece), step)
                copies.append(
                    pltpu.make_async_copy(
                        stage.at[pl.ds(at, step)],
                        out_ref.at[pl.ds(target, step)],
                        sems.at[len(copies)],
                    )
                )
                if len(copies) > 1:
                    copies[-2].start()
    copies[-1].start()
    for copy in copies:
        copy.wait()


def out_call(origins, orders, pairs, core, parts, scores, log_total):
    columns = log_total.shape[1]
    rows = sum(score.shape[0] for score in scores)
    height = rows // len(origins)
    step = math.gcd(parts[0].shape[1], 64)
    return pl.pallas_call(
        functools.partial(out_kernel, origins, orders, pairs, core, height),
        out_shape=jax.ShapeDtypeStruct((rows, columns), jnp.float32),
        in_specs=[VMEM] * (len(parts) + len(scores) + 1),
        out_specs=pl.BlockSpec(memory_space=pl.ANY),
        scratch_shapes=[
            pltpu.VMEM((rows, columns), jnp.float32),
            pltpu.SemaphoreType.DMA((rows // step,)),
        ],
        compiler_params=params(16),
        name="out",
        cost_estimate=pl.CostEstimate(
            flops=3 * rows * columns, bytes_accessed=8 * rows * columns, transcendentals=0
        ),
    )(*parts, *scores, log_total)


def after(value, token):
    return lax.optimization_barrier((value, token))[0]


def chunk_sizes(rows):
    if rows % 128:
        return [rows]
    first, second, last = rows * 11 // 32 // 16 * 16, rows * 11 // 32 // 16 * 16, rows // 8
    return [first, second, rows - first - second - last, last]


def per_device(gallery, querybank, test_queries):
    bank = querybank[0]
    test = test_queries[0]
    gal = lax.axis_size("gal")
    groups = lax.axis_size("qb")
    core = 2 if gal % 2 == 0 else 1
    pairs = gal // core

    def shift(value, pair, flip):
        moves = [
            (i, (i // core + pair) % pairs * core + (i % core ^ flip)) for i in range(gal)
        ]
        return lax.ppermute(value, "gal", moves)

    sizes = chunk_sizes(bank.shape[0])
    starts = [sum(sizes[:i]) for i in range(len(sizes))]
    chunks = cut_call(bank, starts[:1], sizes[:1])
    if len(sizes) > 1:
        chunks += cut_call(bank, starts[1:], sizes[1:])

    crossed = []
    for chunk in chunks:
        crossed += [shift(chunk, pair, 0) for pair in range(1, pairs)]
    test_crossed = [shift(test, pair, 0) for pair in range(1, pairs)]

    near, near_tests = [*chunks], [test]
    if core == 2:
        near.append(shift(bank, 0, 1))
        near_tests.append(shift(test, 0, 1))
    gallery_unit = unit_call(gallery)
    total = bank_call(near, gallery_unit)
    summed = total
    tables = [test_call(near_tests, after(gallery_unit, total))]
    total = after(total, tables[0][0])

    behind = [total]
    for index, block in enumerate(crossed):
        blocks = [after(block, behind[index // 2 * 2] if index else summed)]
        if core == 2:
            blocks.append(shift(blocks[0], 0, 1))
        behind.append(bank_call(blocks, gallery_unit, [behind[-1]]))
    total = behind[-1]

    totals = [total]
    for s in range(1, groups):
        totals.append(
            lax.ppermute(total, "qb", [(i, (i + s) % groups) for i in range(groups)])
        )
    totals[0] = keep_call(total)
    for block in test_crossed:
        block = after(block, totals[0])
        blocks = [block]
        if core == 2:
            blocks.append(shift(block, 0, 1))
        for part in blocks:
            tables.append(test_call([part], gallery_unit))
    scores = [score for score, _ in tables]
    width = math.gcd(test.shape[0], LANES)
    total, part = row_call(totals, [power for _, power in tables], width)

    origins = [(pair, flip) for pair in range(pairs) for flip in range(core)]
    parts = [part]
    orders = [list(range(len(origins)))]
    for pair, flip in origins[1:]:
        parts.append(shift(part, pair, flip))
        orders.append(
            [origins.index(((p - pair) % pairs, f ^ flip)) for p, f in origins]
        )
    log_total, normalizer = log_call(total)
    logprob = out_call(origins, orders, pairs, core, parts, scores, log_total)
    return (logprob, normalizer.reshape(-1))


def solution(mesh):
    placed = (
        P(("slab", "gal"), None),
        P(("slab", "qb"), "gal", None),
        P(("slab", "qb"), "gal", None),
    )

    return jax.shard_map(
        per_device,
        mesh=mesh,
        in_specs=placed,
        out_specs=(P(("slab", "qb"), "gal"), P(("slab", "gal"))),
        check_vma=False,
    )
```

```python
import functools
import math

import jax
import jax.numpy as jnp
from jax import lax
from jax.experimental import pallas as pl
from jax.experimental.pallas import tpu as pltpu
from jax.sharding import PartitionSpec as P


sharpness = 20.0
LOG2E = math.log2(math.e)
LANES = 128


VMEM = pl.BlockSpec(memory_space=pltpu.VMEM)


def params(mib):
    return pltpu.CompilerParams(vmem_limit_bytes=mib << 20)


def unit_rows(values):
    wide = values.astype(jnp.float32)
    scaled = wide * lax.rsqrt(jnp.sum(wide * wide, axis=-1, keepdims=True) + 1e-06)
    return scaled.astype(jnp.bfloat16)


def inner(rows, columns):
    return lax.dot_general(
        rows, columns, (((1,), (0,)), ((), ())), preferred_element_type=jnp.float32
    )


def cut_kernel(starts, source_ref, *refs):
    outs, sems = refs[:-1], refs[-1]
    copies = [
        pltpu.make_async_copy(source_ref.at[pl.ds(start, out.shape[0])], out, sems.at[index])
        for index, (start, out) in enumerate(zip(starts, outs))
    ]
    for copy in copies:
        copy.start()
    for copy in copies:
        copy.wait()


def cut_call(source, starts, sizes):
    shapes = [jax.ShapeDtypeStruct((size, source.shape[1]), source.dtype) for size in sizes]
    return pl.pallas_call(
        functools.partial(cut_kernel, starts),
        out_shape=shapes,
        in_specs=[pl.BlockSpec(memory_space=pltpu.HBM)],
        out_specs=[VMEM] * len(sizes),
        scratch_shapes=[pltpu.SemaphoreType.DMA((len(sizes),))],
        compiler_params=params(4),
        name="cut",
        cost_estimate=pl.CostEstimate(
            flops=0, bytes_accessed=4 * sum(sizes) * source.shape[1], transcendentals=0
        ),
    )(source)


def unit_kernel(step, values_ref, unit_ref, stage, sems):
    rows = values_ref.shape[0]
    copies = [
        pltpu.make_async_copy(
            values_ref.at[pl.ds(start, step)], stage.at[pl.ds(start, step)], sems.at[start // step]
        )
        for start in range(0, rows, step)
    ]
    for copy in copies:
        copy.start()
    for start, copy in zip(range(0, rows, step), copies):
        copy.wait()
        unit_ref[:, start : start + step] = unit_rows(stage[start : start + step, :]).T


def unit_call(values):
    step = math.gcd(values.shape[0], 512)
    return pl.pallas_call(
        functools.partial(unit_kernel, step),
        out_shape=jax.ShapeDtypeStruct(values.shape[::-1], jnp.bfloat16),
        in_specs=[pl.BlockSpec(memory_space=pltpu.HBM)],
        out_specs=VMEM,
        scratch_shapes=[
            pltpu.VMEM(values.shape, values.dtype),
            pltpu.SemaphoreType.DMA((values.shape[0] // step,)),
        ],
        compiler_params=params(16),
        name="unit",
        cost_estimate=pl.CostEstimate(
            flops=4 * values.size, bytes_accessed=4 * values.size, transcendentals=values.shape[0]
        ),
    )(pltpu.with_memory_space_constraint(values, pltpu.HBM))


def bank_kernel(count, tile, *refs):
    blocks, gallery_ref, earlier, total_ref = (
        refs[:count],
        refs[count],
        refs[count + 1 : -1],
        refs[-1],
    )
    units = [unit_rows(block[...]) for block in blocks]
    unit = jnp.concatenate(units, axis=0) if count > 1 else units[0]
    for start in range(0, gallery_ref.shape[1], tile):
        scores = inner(unit, gallery_ref[:, start : start + tile])
        total = jnp.sum(jnp.exp2(scores * (sharpness * LOG2E)), axis=0, keepdims=True)
        for other in earlier:
            total = total + other[:, start : start + tile]
        total_ref[:, start : start + tile] = total


def bank_call(blocks, gallery_unit, earlier=()):
    depth, columns = gallery_unit.shape
    rows = sum(block.shape[0] for block in blocks)
    tile = math.gcd(columns, 256)
    return pl.pallas_call(
        functools.partial(bank_kernel, len(blocks), tile),
        out_shape=jax.ShapeDtypeStruct((1, columns), jnp.float32),
        in_specs=[VMEM] * (len(blocks) + 1 + len(earlier)),
        out_specs=VMEM,
        compiler_params=params(16),
        name="bank",
        cost_estimate=pl.CostEstimate(
            flops=2 * rows * columns * depth,
            bytes_accessed=2 * depth * (rows + columns),
            transcendentals=rows * columns,
        ),
    )(*blocks, gallery_unit, *earlier)


def test_kernel(count, tile, *refs):
    blocks, gallery_ref, (score_ref, power_ref) = refs[:count], refs[count], refs[-2:]
    units = [unit_rows(block[...]) for block in blocks]
    unit = jnp.concatenate(units, axis=0) if count > 1 else units[0]
    for start in range(0, gallery_ref.shape[1], tile):
        scores = inner(unit, gallery_ref[:, start : start + tile])
        score_ref[:, start : start + tile] = scores * sharpness
        power_ref[:, start : start + tile] = jnp.exp2(scores * (sharpness * LOG2E))


def test_call(blocks, gallery_unit):
    depth, columns = gallery_unit.shape
    rows = sum(block.shape[0] for block in blocks)
    tile = math.gcd(columns, 256)
    shape = jax.ShapeDtypeStruct((rows, columns), jnp.float32)
    return pl.pallas_call(
        functools.partial(test_kernel, len(blocks), tile),
        out_shape=(shape, shape),
        in_specs=[VMEM] * (len(blocks) + 1),
        out_specs=(VMEM, VMEM),
        compiler_params=params(16),
        name="test",
        cost_estimate=pl.CostEstimate(
            flops=2 * rows * columns * depth,
            bytes_accessed=2 * depth * (rows + columns) + 8 * rows * columns,
            transcendentals=rows * columns,
        ),
    )(*blocks, gallery_unit)


def keep_kernel(total_ref, kept_ref):
    kept_ref[...] = total_ref[...]


def keep_call(total):
    return pl.pallas_call(
        keep_kernel,
        out_shape=jax.ShapeDtypeStruct(total.shape, total.dtype),
        in_specs=[VMEM],
        out_specs=VMEM,
        compiler_params=params(16),
        name="keep",
        cost_estimate=pl.CostEstimate(
            flops=total.size, bytes_accessed=8 * total.size, transcendentals=0
        ),
    )(total)


def row_kernel(groups, *refs):
    totals, powers, (total_ref, rows_ref, inverse_ref) = (
        refs[:groups],
        refs[groups:-3],
        refs[-3:],
    )
    total = totals[0][...]
    for other in totals[1:]:
        total = total + other[...]
    total_ref[...] = total
    inverse_ref[...] = 1.0 / total
    width = rows_ref.shape[1]
    place = 0
    for power_ref in powers:
        for first in range(0, power_ref.shape[0], width):
            running = jnp.zeros((width, LANES), jnp.float32)
            for start in range(0, total_ref.shape[1], LANES):
                cut = slice(start, start + LANES)
                running = running + power_ref[first : first + width, cut] * inverse_ref[:, cut]
            rows_ref[place : place + 1, :] = jnp.sum(running.T, axis=0, keepdims=True)
            place += 1


def row_call(totals, powers, width):
    columns = powers[0].shape[1]
    rows = sum(power.shape[0] for power in powers)
    return pl.pallas_call(
        functools.partial(row_kernel, len(totals)),
        out_shape=(
            jax.ShapeDtypeStruct((1, columns), jnp.float32),
            jax.ShapeDtypeStruct((rows // width, width), jnp.float32),
        ),
        in_specs=[VMEM] * (len(totals) + len(powers)),
        out_specs=(VMEM, VMEM),
        scratch_shapes=[pltpu.VMEM((1, columns), jnp.float32)],
        compiler_params=params(16),
        name="rows",
        cost_estimate=pl.CostEstimate(
            flops=2 * rows * columns, bytes_accessed=4 * rows * columns, transcendentals=0
        ),
    )(*totals, *powers)


def log_kernel(total_ref, *refs):
    scores, log_ref, outs = refs[: len(refs) // 2], refs[len(refs) // 2], refs[len(refs) // 2 + 1 :]
    log_ref[...] = jnp.log(total_ref[...])
    for score_ref, out_ref in zip(scores, outs):
        height, columns = score_ref.shape
        for first in range(0, height, 64):
            for start in range(0, columns, LANES):
                cut = slice(start, start + LANES)
                rows = slice(first, min(first + 64, height))
                out_ref[rows, cut] = score_ref[rows, cut] - log_ref[:, cut]


def log_call(total, scores):
    shapes = [jax.ShapeDtypeStruct(one.shape, jnp.float32) for one in (total, *scores)]
    return pl.pallas_call(
        log_kernel,
        out_shape=shapes,
        in_specs=[VMEM] * len(shapes),
        out_specs=[VMEM] * len(shapes),
        compiler_params=params(16),
        name="logs",
        cost_estimate=pl.CostEstimate(
            flops=total.size, bytes_accessed=12 * total.size, transcendentals=total.size
        ),
    )(total, *scores)


def out_kernel(origins, orders, pairs, core, height, *refs):
    count = len(origins)
    parts, scores, (out_ref, stage, sems) = refs[:count], refs[count:-3], refs[-3:]
    width = parts[0].shape[1]
    line = height // width
    step = math.gcd(width, 32)
    where = lax.axis_index("gal")
    pair_at, core_at = lax.div(where, core), lax.rem(where, core)
    rows_of = [(score, first) for score in scores for first in range(0, score.shape[0], height)]
    copies = []
    for block, (pair, flip) in enumerate(origins):
        side = core_at if flip == 0 else 1 - core_at
        place = (lax.rem(pair_at + (pairs - pair), pairs) * core + side) * height
        source, first = rows_of[block]
        for sub in range(0, height, width):
            total = None
            for part, order in zip(parts, orders):
                at = order[block] * line + sub // width
                row = part[at : at + 1, :]
                total = row if total is None else total + row
            wide = jnp.broadcast_to(jnp.log(total), (LANES, width)).T
            for piece in range(0, width, step):
                at = len(copies) * step
                begin = first + sub + piece
                for start in range(0, stage.shape[1], LANES):
                    cut = slice(start, start + LANES)
                    value = source[begin : begin + step, cut]
                    stage[at : at + step, cut] = value - wide[piece : piece + step, :]
                target = pl.multiple_of(place + (sub + piece), step)
                copies.append(
                    pltpu.make_async_copy(
                        stage.at[pl.ds(at, step)],
                        out_ref.at[pl.ds(target, step)],
                        sems.at[len(copies)],
                    )
                )
                if len(copies) > 1:
                    copies[-2].start()
    copies[-1].start()
    for copy in copies:
        copy.wait()


def out_call(origins, orders, pairs, core, parts, scores):
    columns = scores[0].shape[1]
    rows = sum(score.shape[0] for score in scores)
    height = rows // len(origins)
    step = math.gcd(parts[0].shape[1], 32)
    return pl.pallas_call(
        functools.partial(out_kernel, origins, orders, pairs, core, height),
        out_shape=jax.ShapeDtypeStruct((rows, columns), jnp.float32),
        in_specs=[VMEM] * (len(parts) + len(scores)),
        out_specs=pl.BlockSpec(memory_space=pl.ANY),
        scratch_shapes=[
            pltpu.VMEM((rows, columns), jnp.float32),
            pltpu.SemaphoreType.DMA((rows // step,)),
        ],
        compiler_params=params(16),
        name="out",
        cost_estimate=pl.CostEstimate(
            flops=3 * rows * columns, bytes_accessed=8 * rows * columns, transcendentals=0
        ),
    )(*parts, *scores)


def after(value, token):
    return lax.optimization_barrier((value, token))[0]


def chunk_sizes(rows):
    if rows % 128:
        return [rows]
    first, second, last = rows * 10 // 32 // 16 * 16, rows * 11 // 32 // 16 * 16, rows // 8
    return [first, second, rows - first - second - last, last]


def per_device(gallery, querybank, test_queries):
    bank = querybank[0]
    test = test_queries[0]
    gal = lax.axis_size("gal")
    groups = lax.axis_size("qb")
    core = 2 if gal % 2 == 0 else 1
    pairs = gal // core

    def shift(value, pair, flip):
        moves = [
            (i, (i // core + pair) % pairs * core + (i % core ^ flip)) for i in range(gal)
        ]
        return lax.ppermute(value, "gal", moves)

    sizes = chunk_sizes(bank.shape[0])
    starts = [sum(sizes[:i]) for i in range(len(sizes))]
    chunks = cut_call(bank, starts[:1], sizes[:1])
    if len(sizes) > 1:
        chunks += cut_call(bank, starts[1:], sizes[1:])

    crossed = []
    for chunk in chunks:
        crossed += [shift(chunk, pair, 0) for pair in range(1, pairs)]
    test_crossed = [shift(test, pair, 0) for pair in range(1, pairs)]

    near, near_tests = [*chunks], [test]
    if core == 2:
        near.append(shift(bank, 0, 1))
        near_tests.append(shift(test, 0, 1))
    gallery_unit = unit_call(gallery)
    total = bank_call(near, gallery_unit)
    summed = total
    tables = [test_call(near_tests, after(gallery_unit, total))]
    total = after(total, tables[0][0])

    behind = [total]
    for index, block in enumerate(crossed):
        blocks = [after(block, behind[index // 2 * 2] if index else summed)]
        if core == 2:
            blocks.append(shift(blocks[0], 0, 1))
        behind.append(bank_call(blocks, gallery_unit, [behind[-1]]))
    total = behind[-1]

    totals = [total]
    for s in range(1, groups):
        totals.append(
            lax.ppermute(total, "qb", [(i, (i + s) % groups) for i in range(groups)])
        )
    totals[0] = keep_call(total)
    for block in test_crossed:
        block = after(block, totals[0])
        blocks = [block]
        if core == 2:
            blocks.append(shift(block, 0, 1))
        for part in blocks:
            tables.append(test_call([part], gallery_unit))
    scores = [score for score, _ in tables]
    width = math.gcd(test.shape[0], LANES)
    total, part = row_call(totals, [power for _, power in tables], width)

    origins = [(pair, flip) for pair in range(pairs) for flip in range(core)]
    parts = [part]
    orders = [list(range(len(origins)))]
    for pair, flip in origins[1:]:
        parts.append(shift(part, pair, flip))
        orders.append(
            [origins.index(((p - pair) % pairs, f ^ flip)) for p, f in origins]
        )
    normalizer, *scores = log_call(total, scores)
    logprob = out_call(origins, orders, pairs, core, parts, scores)
    return (logprob, normalizer.reshape(-1))


def solution(mesh):
    placed = (
        P(("slab", "gal"), None),
        P(("slab", "qb"), "gal", None),
        P(("slab", "qb"), "gal", None),
    )

    return jax.shard_map(
        per_device,
        mesh=mesh,
        in_specs=placed,
        out_specs=(P(("slab", "qb"), "gal"), P(("slab", "gal"))),
        check_vma=False,
    )
```
